32 devices in a mesh: az: 4 (over x, core), rad: 8 (over z, y).
Axes of the slice: x: 2, y: 2, z: 4, core: 2. Of those that a mesh axis runs over, the one named last changes fastest.
Arguments:
- fields: float32 [4, 16, 64, 512], P(None, None, 'rad', 'az'), may hold values from -6 to 6, as said below
- shifts: int32 [16, 64], P(None, 'rad'), may hold values from 0 to 511, as said below
- courant: float32 [16, 64], P(None, 'rad'), may hold values from -0.45 to 0.45
Outputs:
- advanced: float32 [4, 16, 64, 512], P(None, None, 'rad', 'az')
The draws below stay inside these ranges and needn't reach their ends.
Inputs may be any that keep to these rules, and one draw needn't show every extreme that they name: fields 0 and 1 (velocities) lie in the range; fields 2 and 3 (energy, density) lie between 0.5 and 2. `shifts`: any whole shift of a cycle in cells.
All inputs are finite; a program needn't handle non-finite values.
Results may differ from the reference program's by a relative error of at most 0.0003.
Values sent between devices are 32-bit elements; how exact they have to be, the bound alone decides.
A program may use at most 64 MiB of HBM per device.

```python
import math
import jax
import jax.numpy as jnp
from jax import lax

NTH = 16
NPHI = 512
NR = 64


def draw_fields(key, part):
    keys = jax.random.split(jax.random.fold_in(key, 11), 2)
    low = math.log(0.5)
    high = math.log(2.0)
    velocity = jax.random.truncated_normal(keys[0], -6.0, 6.0, (2, NTH, NR, NPHI), jnp.float32)
    positive = jnp.exp(jax.random.uniform(keys[1], (2, NTH, NR, NPHI), jnp.float32, low, high))
    return jnp.concatenate([velocity, positive], axis=0)


def draw_shifts(key, part):
    values = jax.random.randint(jax.random.fold_in(key, 23), (NTH, NR), 0, NPHI, jnp.int32)
    values = values.at[0, 0].set(NPHI - 1)
    return values.at[0, 1].set(0)


def shard_levels(stream_key, dims, shards, least, high):
    loudness = 1.0
    for position, parts in shards:
        heights = jax.random.uniform(jax.random.fold_in(jax.random.fold_in(stream_key, 6), position), (parts,), jnp.float32, least / len(shards), high / len(shards))
        loudness = loudness * jnp.repeat(jnp.exp(heights), dims[position] // parts).reshape((-1,) + (1,) * (len(dims) - 1 - position))
    return loudness


def setup_inputs(seed: int = 0) -> dict:
    seeds = jax.random.split(jax.random.key(seed), 4)
    fields = draw_fields(jax.random.fold_in(seeds[3], 71), 0)
    shifts = draw_shifts(jax.random.fold_in(seeds[3], 71), 0)
    courant = jnp.clip(jax.random.uniform(seeds[2], (NTH, NR), jnp.float32, -0.45, 0.45) * shard_levels(seeds[2], (NTH, NR), ((1, 8),), -0.4, 0.0), -0.45, 0.45)
    return dict(fields=fields, shifts=shifts, courant=courant)


inner_radius = 0.4
adiabatic = 1.4


def minmod(left, right):
    return 0.5 * (jnp.sign(left) + jnp.sign(right)) * jnp.minimum(jnp.abs(left), jnp.abs(right))


def limited(extended, courant_cycle):
    differences = extended[..., 1:] - extended[..., :-1]
    slopes = minmod(differences[..., :-1], differences[..., 1:])
    centers = extended[..., 1:-1]
    flux_plus = courant_cycle * (centers[..., :-1] + 0.5 * (1.0 - courant_cycle) * slopes[..., :-1])
    flux_minus = courant_cycle * (centers[..., 1:] - 0.5 * (1.0 + courant_cycle) * slopes[..., 1:])
    face_flux = jnp.where(courant_cycle >= 0.0, flux_plus, flux_minus)
    return extended[..., 2:-2] - (face_flux[..., 1:] - face_flux[..., :-1])


def center(field):
    return field[..., 1:-1, 1:-1]


def across_az(field):
    return field[..., 1:-1, 2:] - field[..., 1:-1, :-2]


def across_rad(field):
    return field[..., 2:, 1:-1] - field[..., :-2, 1:-1]


def laplace(field, phi_width, rad_step):
    middle = center(field)
    along_az = (field[..., 1:-1, 2:] + field[..., 1:-1, :-2] - 2.0 * middle) / (phi_width * phi_width)
    along_rad = (field[..., 2:, 1:-1] + field[..., :-2, 1:-1] - 2.0 * middle) / (rad_step * rad_step)
    return along_az + along_rad


def stencil(padded, density, radius, phi_count, rad_count):
    phi_step = 2.0 * math.pi / phi_count
    rad_step = 1.0 / rad_count
    spacing = min(rad_step, inner_radius * phi_step)
    time_step = 0.2 * spacing
    viscosity = 0.05 * spacing * spacing / time_step
    radial_vel = padded[0]
    azim_vel = padded[1]
    energy = padded[2]
    pressure = (adiabatic - 1.0) * energy
    phi_width = radius * phi_step
    radial_mid = center(radial_vel)
    azim_mid = center(azim_vel)
    energy_mid = center(energy)
    radial_new = radial_mid + time_step * (-across_rad(pressure) * (0.5 / rad_step) / density
                                           + viscosity * laplace(radial_vel, phi_width, rad_step)
                                           + azim_mid * azim_mid / radius - 1.0 / (radius * radius))
    azim_new = azim_mid + time_step * (-across_az(pressure) * 0.5 / (phi_width * density)
                                       + viscosity * laplace(azim_vel, phi_width, rad_step)
                                       - radial_mid * azim_mid / radius)
    divergence = across_rad(radial_vel) * (0.5 / rad_step) + across_az(azim_vel) * 0.5 / phi_width + radial_mid / radius
    energy_new = energy_mid - time_step * (adiabatic - 1.0) * energy_mid * divergence
    return radial_new, azim_new, energy_new


def reference(fields, shifts, courant):
    radius = (inner_radius + (jnp.arange(NR).astype(jnp.float32) + 0.5) * (1.0 / NR))[:, None]

    def one_slice(inputs):
        slab, cycle_shift, cycle_courant = inputs
        padded = jnp.pad(slab[0:3], ((0, 0), (1, 1), (0, 0)), mode="edge")
        padded = jnp.concatenate([padded[..., -1:], padded, padded[..., :1]], axis=-1)
        radial_new, azim_new, energy_new = stencil(padded, slab[3], radius, NPHI, NR)
        moved = jnp.stack([radial_new, azim_new, energy_new, slab[3]])
        take_index = (jnp.arange(NPHI).astype(jnp.int32)[None, :] - cycle_shift[:, None]) % NPHI
        take_index = jnp.broadcast_to(take_index[None], moved.shape)
        shifted = jnp.take_along_axis(moved, take_index, axis=-1)
        extended = jnp.concatenate([shifted[..., -2:], shifted, shifted[..., :2]], axis=-1)
        return limited(extended, cycle_courant[None, :, None])

    advanced = lax.map(one_slice, (jnp.moveaxis(fields, 1, 0), shifts, courant))
    return jnp.moveaxis(advanced, 0, 1)
```

```python
import functools
import math

import jax
import jax.numpy as jnp
from jax import lax
from jax.experimental import pallas as pl
from jax.experimental.pallas import tpu as pltpu
from jax.sharding import PartitionSpec as P

inner_radius = 0.4
adiabatic = 1.4
MESH = pl.DeviceIdType.MESH
OFFSETS = (-2, -1, 0, 1)
CHUNKS = 4


def remote(src, dst, send, recv, az, rad):
    return pltpu.make_async_remote_copy(
        src_ref=src,
        dst_ref=dst,
        send_sem=send,
        recv_sem=recv,
        device_id={"az": az, "rad": rad},
        device_id_type=MESH,
    )


def minmod(a, b):
    return jnp.maximum(jnp.minimum(a, b), 0.0) + jnp.minimum(jnp.maximum(a, b), 0.0)


def kernel(n, rn, fields, shifts, courant, out, G, H, E, SEG, LANE, CA,
           local_sem, xs, xr, hs, hr, cs, cr, fs, fr):
    _, T, R, L = fields.shape
    X = n // 2
    K = xs.shape[0]
    tc = T // K
    az = lax.axis_index("az")
    rad = lax.axis_index("rad")
    x, c = az // 2, az % 2
    mate = x * 2 + (1 - c)

    def column(k):
        return lax.rem(x + k, X) * 2 + c

    def source(k, core):
        return lax.rem(x + X - k, X) * 2 + core

    has_low, has_high = rad > 0, rad < rn - 1
    sends = (has_high, has_low)
    receives = (has_low, has_high)
    toward = (rad + 1, rad - 1)

    local = pltpu.make_async_copy(fields, G.at[az], local_sem)
    local.start()

    barrier = pltpu.get_barrier_semaphore()

    def greet(a, r):
        pl.semaphore_signal(barrier, inc=1, device_id={"az": a, "rad": r}, device_id_type=MESH)

    greet(mate, rad)
    for k in range(1, X):
        greet(column(k), rad)
    for way in range(2):
        @pl.when(sends[way])
        def _():
            for k in range(X):
                greet(column(k), toward[way])
    neighbours = has_low.astype(jnp.int32) + has_high.astype(jnp.int32)

    local.wait()
    for f in range(3):
        E[0, f] = G[az, f, :, R - 1, :]
        E[1, f] = G[az, f, :, 0, :]

    pl.semaphore_wait(barrier, X + X * neighbours)

    def block(ref, seg, j):
        return ref.at[seg, :, pl.ds(j * tc, tc)]

    def field_copy(j, k):
        return remote(block(G, az, j), block(G, az, j), xs.at[j, k - 1], xr.at[j, k - 1], column(k), rad)

    def field_arrival(j, k):
        seg = source(k, c)
        return remote(block(G, seg, j), block(G, seg, j), xs.at[j, k - 1], xr.at[j, k - 1], column(k), rad)

    def edge_copy(way, k):
        return remote(E.at[way], H.at[way, az], hs.at[way, k], hr.at[way, k], column(k), toward[way])

    def edge_arrival(way, k):
        return remote(E.at[way], H.at[way, source(k, c)], hs.at[way, k], hr.at[way, k], column(k), rad)

    def mate_copy(j, k):
        seg = source(k, c)
        return remote(block(G, seg, j), block(G, seg, j), cs.at[j, k], cr.at[j, k], mate, rad)

    def mate_arrival(j, k):
        seg = source(k, 1 - c)
        return remote(block(G, seg, j), block(G, seg, j), cs.at[j, k], cr.at[j, k], mate, rad)

    def mate_edge(way, k):
        seg = source(k, c)
        return remote(H.at[way, seg], H.at[way, seg], fs.at[way, k], fr.at[way, k], mate, rad)

    def mate_edge_arrival(way, k):
        seg = source(k, 1 - c)
        return remote(H.at[way, seg], H.at[way, seg], fs.at[way, k], fr.at[way, k], mate, rad)

    for way in range(2):
        @pl.when(sends[way])
        def _():
            for k in range(X - 1, -1, -1):
                edge_copy(way, k).start()
    for j in range(K):
        for k in range(1, X):
            field_copy(j, k).start()
    for j in range(K):
        mate_copy(j, 0).start()

    for way in range(2):
        @pl.when(jnp.logical_not(receives[way]))
        def _():
            H[way] = jnp.zeros(H.shape[1:], jnp.float32)

    phi_count, rad_count = n * L, rn * R
    phi_step = 2.0 * math.pi / phi_count
    rad_step = 1.0 / rad_count
    spacing = min(rad_step, inner_radius * phi_step)
    dt = 0.2 * spacing
    viscosity = 0.05 * spacing * spacing / dt
    row = lax.broadcasted_iota(jnp.int32, (R, L), 0)
    lane = lax.broadcasted_iota(jnp.int32, (R, L), 1)
    radius = inner_radius + ((rad * R + row).astype(jnp.float32) + 0.5) * (1.0 / rad_count)
    width = radius * phi_step
    inv_r = 1.0 / radius
    inv_w = 1.0 / width
    spread_az = (dt * viscosity) * inv_w * inv_w
    spread_rad = dt * viscosity / (rad_step * rad_step)
    press_rad = dt * (adiabatic - 1.0) * 0.5 / rad_step
    press_az = (dt * (adiabatic - 1.0) * 0.5) * inv_w
    turn = dt * inv_r
    pull = dt * inv_r * inv_r
    heat = dt * (adiabatic - 1.0)
    heat_rad = heat * 0.5 / rad_step
    heat_az = (heat * 0.5) * inv_w
    heat_r = heat * inv_r
    bits = L.bit_length() - 1

    diagonal = lax.broadcasted_iota(jnp.int32, (R, R), 0) == lax.broadcasted_iota(jnp.int32, (R, R), 1)

    def as_column(values):
        spread = jnp.where(diagonal, jnp.broadcast_to(values, (R, R)), 0.0)
        return jnp.broadcast_to(jnp.sum(spread, axis=1, keepdims=True), (R, L))

    def prepare(t, carry):
        moves = as_column(shifts[pl.ds(t, 1), :].astype(jnp.float32)).astype(jnp.int32)
        cour = as_column(courant[pl.ds(t, 1), :])
        CA[t] = jnp.abs(cour)
        sign = jnp.where(cour >= 0.0, 1, -1)
        for o, offset in enumerate(OFFSETS):
            s = moves - sign * offset
            s = jnp.where(s < 0, s + phi_count, s)
            s = jnp.where(s >= phi_count, s - phi_count, s)
            q = s >> bits
            rest = s & (L - 1)
            seg = az - q - jnp.where(lane + rest >= L, 1, 0)
            SEG[t, o] = jnp.where(seg < 0, seg + n, seg)
            LANE[t, o] = (lane - rest) & (L - 1)
        return carry

    lax.fori_loop(0, T, prepare, 0)

    first_lane, last_lane = lane == 0, lane == L - 1
    low_own = (row == 0) & jnp.logical_not(has_low)
    high_own = (row == R - 1) & jnp.logical_not(has_high)
    low_halo = (row == 0) & has_low
    high_halo = (row == R - 1) & has_high

    def step(t, carry):
        raw = [[G[s, f, t] for f in range(4)] for s in range(n)]
        moved = []
        for s in range(n):
            before, here, after = raw[s - 1], raw[s], raw[(s + 1) % n]
            vr, vp, en, den = here

            def around(f):
                q = here[f]
                left = pltpu.roll(jnp.where(last_lane, before[f], q), 1, 1)
                right = pltpu.roll(jnp.where(first_lane, after[f], q), L - 1, 1)
                low = jnp.where(low_own, q, pltpu.roll(q, 1, 0))
                low = jnp.where(low_halo, H[0, s, f, pl.ds(t, 1), :], low)
                high = jnp.where(high_own, q, pltpu.roll(q, R - 1, 0))
                high = jnp.where(high_halo, H[1, s, f, pl.ds(t, 1), :], high)
                return left, right, low, high

            vl, vh, vd, vu = around(0)
            pl_, ph, pd, pu = around(1)
            el, eh, ed, eu = around(2)
            inv_den = 1.0 / den
            new_r = vr + (
                spread_az * (vh + vl - 2.0 * vr)
                + spread_rad * (vu + vd - 2.0 * vr)
                + (vp * vp * turn - pull)
                - press_rad * (eu - ed) * inv_den
            )
            new_p = vp + (
                spread_az * (ph + pl_ - 2.0 * vp)
                + spread_rad * (pu + pd - 2.0 * vp)
                - vr * vp * turn
                - press_az * (eh - el) * inv_den
            )
            new_e = en - en * (heat_rad * (vu - vd) + heat_az * (ph - pl_) + heat_r * vr)
            moved.append((new_r, new_p, new_e, den))
        amount = CA[t]
        half = 0.5 * (1.0 - amount)
        taken = [[] for _ in range(4)]
        for o in range(len(OFFSETS)):
            seg, at = SEG[t, o], LANE[t, o]
            chosen = [seg == s for s in range(n - 1)]
            for f in range(4):
                value = moved[n - 1][f]
                for s in range(n - 1):
                    value = jnp.where(chosen[s], moved[s][f], value)
                taken[f].append(jnp.take_along_axis(value, at, axis=1, mode="promise_in_bounds"))
        for f in range(4):
            q0, q1, q2, q3 = taken[f]
            d0, d1, d2 = q1 - q0, q2 - q1, q3 - q2
            enters = q1 + half * minmod(d0, d1)
            leaves = q2 + half * minmod(d1, d2)
            out[f, t] = q2 - amount * (leaves - enters)
        return carry

    def finish(j):
        for k in range(X):
            mate_arrival(j, k).wait_recv()
        lax.fori_loop(j * tc, (j + 1) * tc, step, 0)

    for way in range(2):
        @pl.when(receives[way])
        def _():
            for k in range(X):
                edge_arrival(way, k).wait_recv()
                mate_edge(way, k).start()
    for j in range(K):
        for k in range(1, X):
            field_arrival(j, k).wait_recv()
            mate_copy(j, k).start()
        if j == 0:
            for way in range(2):
                @pl.when(receives[way])
                def _():
                    for k in range(X):
                        mate_edge_arrival(way, k).wait_recv()
        else:
            finish(j - 1)
    finish(K - 1)

    for way in range(2):
        @pl.when(sends[way])
        def _():
            for k in range(X):
                edge_copy(way, k).wait_send()

        @pl.when(receives[way])
        def _():
            for k in range(X):
                mate_edge(way, k).wait_send()
    for j in range(K):
        for k in range(1, X):
            field_copy(j, k).wait_send()
        for k in range(X):
            mate_copy(j, k).wait_send()


def shards(fields, shifts, courant):
    n, rn = lax.axis_size("az"), lax.axis_size("rad")
    F, T, R, L = fields.shape
    X = n // 2
    K = math.gcd(T, CHUNKS)
    dma = pltpu.SemaphoreType.DMA
    vmem = pl.BlockSpec(memory_space=pltpu.VMEM)
    return pl.pallas_call(
        functools.partial(kernel, n, rn),
        out_shape=jax.ShapeDtypeStruct(fields.shape, jnp.float32),
        in_specs=[pl.BlockSpec(memory_space=pl.ANY), vmem, vmem],
        out_specs=vmem,
        scratch_shapes=[
            pltpu.VMEM((n, F, T, R, L), jnp.float32),
            pltpu.VMEM((2, n, 3, T, L), jnp.float32),
            pltpu.VMEM((2, 3, T, L), jnp.float32),
            pltpu.VMEM((T, 4, R, L), jnp.int32),
            pltpu.VMEM((T, 4, R, L), jnp.int32),
            pltpu.VMEM((T, R, L), jnp.float32),
            dma(()),
            dma((K, X - 1)), dma((K, X - 1)),
            dma((2, X)), dma((2, X)),
            dma((K, X)), dma((K, X)),
            dma((2, X)), dma((2, X)),
        ],
        compiler_params=pltpu.CompilerParams(collective_id=0, has_side_effects=True),
    )(fields, shifts, courant)


def solution(mesh):
    return jax.shard_map(
        shards,
        mesh=mesh,
        in_specs=(P(None, None, "rad", "az"), P(None, "rad"), P(None, "rad")),
        out_specs=P(None, None, "rad", "az"),
        check_vma=False,
    )
```

```python
import functools
import math

import jax
import jax.numpy as jnp
from jax import lax
from jax.experimental import pallas as pl
from jax.experimental.pallas import tpu as pltpu
from jax.sharding import PartitionSpec as P

inner_radius = 0.4
adiabatic = 1.4
MESH = pl.DeviceIdType.MESH
OFFSETS = (-2, -1, 0, 1)
CHUNKS = 4


def remote(src, dst, send, recv, az, rad):
    return pltpu.make_async_remote_copy(
        src_ref=src,
        dst_ref=dst,
        send_sem=send,
        recv_sem=recv,
        device_id={"az": az, "rad": rad},
        device_id_type=MESH,
    )


def minmod(a, b):
    return jnp.maximum(jnp.minimum(a, b), 0.0) + jnp.minimum(jnp.maximum(a, b), 0.0)


def kernel(n, rn, fields, shifts_in, courant_in, out, G, H, SEG, LANE, CA, shifts, courant,
           local_sem, small_sem, xs, xr, hs, hr, cs, cr, fs, fr):
    _, T, R, L = fields.shape
    X = n // 2
    K = xs.shape[0]
    tc = T // K
    az = lax.axis_index("az")
    rad = lax.axis_index("rad")
    x, c = az // 2, az % 2
    mate = x * 2 + (1 - c)

    def column(k):
        return lax.rem(x + k, X) * 2 + c

    def source(k, core):
        return lax.rem(x + X - k, X) * 2 + core

    has_low, has_high = rad > 0, rad < rn - 1
    sends = (has_high, has_low)
    receives = (has_low, has_high)
    toward = (rad + 1, rad - 1)

    local = pltpu.make_async_copy(fields, G.at[az], local_sem)
    local.start()
    small = (
        pltpu.make_async_copy(shifts_in, shifts, small_sem.at[0]),
        pltpu.make_async_copy(courant_in, courant, small_sem.at[1]),
    )
    for copy in small:
        copy.start()

    barrier = pltpu.get_barrier_semaphore()

    def greet(a, r):
        pl.semaphore_signal(barrier, inc=1, device_id={"az": a, "rad": r}, device_id_type=MESH)

    greet(mate, rad)
    for k in range(1, X):
        greet(column(k), rad)
    for way in range(2):
        @pl.when(sends[way])
        def _():
            for k in range(X):
                greet(column(k), toward[way])
    neighbours = has_low.astype(jnp.int32) + has_high.astype(jnp.int32)


    pl.semaphore_wait(barrier, X + X * neighbours)

    def block(ref, seg, j):
        return ref.at[seg, :, pl.ds(j * tc, tc)]

    def field_copy(j, k):
        return remote(fields.at[:, pl.ds(j * tc, tc)], block(G, az, j), xs.at[j, k - 1], xr.at[j, k - 1], column(k), rad)

    def field_arrival(j, k):
        seg = source(k, c)
        return remote(block(G, seg, j), block(G, seg, j), xs.at[j, k - 1], xr.at[j, k - 1], column(k), rad)

    def edge_copy(way, k):
        return remote(fields.at[0:3, :, (R - 1) * (1 - way), :], H.at[way, az], hs.at[way, k], hr.at[way, k], column(k), toward[way])

    def edge_arrival(way, k):
        return remote(H.at[way, az], H.at[way, source(k, c)], hs.at[way, k], hr.at[way, k], column(k), rad)

    def mate_copy(j, k):
        seg = source(k, c)
        sent = block(G, seg, j) if k else fields.at[:, pl.ds(j * tc, tc)]
        return remote(sent, block(G, seg, j), cs.at[j, k], cr.at[j, k], mate, rad)

    def mate_arrival(j, k):
        seg = source(k, 1 - c)
        return remote(block(G, seg, j), block(G, seg, j), cs.at[j, k], cr.at[j, k], mate, rad)

    def mate_edge(way, k):
        seg = source(k, c)
        return remote(H.at[way, seg], H.at[way, seg], fs.at[way, k], fr.at[way, k], mate, rad)

    def mate_edge_arrival(way, k):
        seg = source(k, 1 - c)
        return remote(H.at[way, seg], H.at[way, seg], fs.at[way, k], fr.at[way, k], mate, rad)

    for way in range(2):
        @pl.when(sends[way])
        def _():
            for k in range(X - 1, -1, -1):
                edge_copy(way, k).start()
    for j in range(K):
        for k in range(1, X):
            field_copy(j, k).start()
    for j in range(K):
        mate_copy(j, 0).start()

    for way in range(2):
        @pl.when(jnp.logical_not(receives[way]))
        def _():
            H[way] = jnp.zeros(H.shape[1:], jnp.float32)

    phi_count, rad_count = n * L, rn * R
    phi_step = 2.0 * math.pi / phi_count
    rad_step = 1.0 / rad_count
    spacing = min(rad_step, inner_radius * phi_step)
    dt = 0.2 * spacing
    viscosity = 0.05 * spacing * spacing / dt
    row = lax.broadcasted_iota(jnp.int32, (R, L), 0)
    lane = lax.broadcasted_iota(jnp.int32, (R, L), 1)
    radius = inner_radius + ((rad * R + row).astype(jnp.float32) + 0.5) * (1.0 / rad_count)
    width = radius * phi_step
    inv_r = 1.0 / radius
    inv_w = 1.0 / width
    spread_az = (dt * viscosity) * inv_w * inv_w
    spread_rad = dt * viscosity / (rad_step * rad_step)
    press_rad = dt * (adiabatic - 1.0) * 0.5 / rad_step
    press_az = (dt * (adiabatic - 1.0) * 0.5) * inv_w
    turn = dt * inv_r
    pull = dt * inv_r * inv_r
    heat = dt * (adiabatic - 1.0)
    heat_rad = heat * 0.5 / rad_step
    heat_az = (heat * 0.5) * inv_w
    heat_r = heat * inv_r
    bits = L.bit_length() - 1

    local.wait()
    for copy in small:
        copy.wait()
    for t in range(T):
        moves = jnp.broadcast_to(shifts[:, t : t + 1], (R, L))
        cour = jnp.broadcast_to(courant[:, t : t + 1], (R, L))
        CA[t] = jnp.abs(cour)
        sign = jnp.where(cour >= 0.0, 1, -1)
        for o, offset in enumerate(OFFSETS):
            s = moves - sign * offset
            s = jnp.where(s < 0, s + phi_count, s)
            s = jnp.where(s >= phi_count, s - phi_count, s)
            q = s >> bits
            rest = s & (L - 1)
            seg = az - q - jnp.where(lane + rest >= L, 1, 0)
            SEG[t, o] = jnp.where(seg < 0, seg + n, seg)
            LANE[t, o] = (lane - rest) & (L - 1)

    first_lane, last_lane = lane == 0, lane == L - 1
    low_own = (row == 0) & jnp.logical_not(has_low)
    high_own = (row == R - 1) & jnp.logical_not(has_high)
    low_halo = (row == 0) & has_low
    high_halo = (row == R - 1) & has_high

    def step(t, carry):
        raw = [[G[s, f, t] for f in range(4)] for s in range(n)]
        moved = []
        for s in range(n):
            before, here, after = raw[s - 1], raw[s], raw[(s + 1) % n]
            vr, vp, en, den = here

            def around(f):
                q = here[f]
                left = pltpu.roll(jnp.where(last_lane, before[f], q), 1, 1)
                right = pltpu.roll(jnp.where(first_lane, after[f], q), L - 1, 1)
                low = jnp.where(low_own, q, pltpu.roll(q, 1, 0))
                low = jnp.where(low_halo, H[0, s, f, pl.ds(t, 1), :], low)
                high = jnp.where(high_own, q, pltpu.roll(q, R - 1, 0))
                high = jnp.where(high_halo, H[1, s, f, pl.ds(t, 1), :], high)
                return left, right, low, high

            vl, vh, vd, vu = around(0)
            pl_, ph, pd, pu = around(1)
            el, eh, ed, eu = around(2)
            inv_den = 1.0 / den
            new_r = vr + (
                spread_az * (vh + vl - 2.0 * vr)
                + spread_rad * (vu + vd - 2.0 * vr)
                + (vp * vp * turn - pull)
                - press_rad * (eu - ed) * inv_den
            )
            new_p = vp + (
                spread_az * (ph + pl_ - 2.0 * vp)
                + spread_rad * (pu + pd - 2.0 * vp)
                - vr * vp * turn
                - press_az * (eh - el) * inv_den
            )
            new_e = en - en * (heat_rad * (vu - vd) + heat_az * (ph - pl_) + heat_r * vr)
            moved.append((new_r, new_p, new_e, den))
        amount = CA[t]
        half = 0.5 * (1.0 - amount)
        taken = [[] for _ in range(4)]
        for o in range(len(OFFSETS)):
            seg, at = SEG[t, o], LANE[t, o]
            chosen = [seg == s for s in range(n - 1)]
            for f in range(4):
                value = moved[n - 1][f]
                for s in range(n - 1):
                    value = jnp.where(chosen[s], moved[s][f], value)
                taken[f].append(jnp.take_along_axis(value, at, axis=1, mode="promise_in_bounds"))
        for f in range(4):
            q0, q1, q2, q3 = taken[f]
            d0, d1, d2 = q1 - q0, q2 - q1, q3 - q2
            enters = q1 + half * minmod(d0, d1)
            leaves = q2 + half * minmod(d1, d2)
            out[f, t] = q2 - amount * (leaves - enters)
        return carry

    def finish(j):
        for k in range(X):
            mate_arrival(j, k).wait_recv()
        lax.fori_loop(j * tc, (j + 1) * tc, step, 0)

    for way in range(2):
        @pl.when(receives[way])
        def _():
            for k in range(X):
                edge_arrival(way, k).wait_recv()
                mate_edge(way, k).start()
    for j in range(K):
        for k in range(1, X):
            field_arrival(j, k).wait_recv()
            mate_copy(j, k).start()
        if j == 0:
            for way in range(2):
                @pl.when(receives[way])
                def _():
                    for k in range(X):
                        mate_edge_arrival(way, k).wait_recv()
        else:
            finish(j - 1)
    finish(K - 1)

    for way in range(2):
        @pl.when(sends[way])
        def _():
            for k in range(X):
                edge_copy(way, k).wait_send()

        @pl.when(receives[way])
        def _():
            for k in range(X):
                mate_edge(way, k).wait_send()
    for j in range(K):
        for k in range(1, X):
            field_copy(j, k).wait_send()
        for k in range(X):
            mate_copy(j, k).wait_send()


def shards(fields, shifts, courant):
    n, rn = lax.axis_size("az"), lax.axis_size("rad")
    F, T, R, L = fields.shape
    X = n // 2
    K = math.gcd(T, CHUNKS)
    held = (n + 2) * F * T * R * L + 2 * n * 3 * T * L + 9 * T * R * L
    grant = 4 * held + (2 << 20)
    dma = pltpu.SemaphoreType.DMA
    vmem = pl.BlockSpec(memory_space=pltpu.VMEM)
    return pl.pallas_call(
        functools.partial(kernel, n, rn),
        out_shape=jax.ShapeDtypeStruct(fields.shape, jnp.float32),
        in_specs=[pl.BlockSpec(memory_space=pltpu.HBM)] * 3,
        out_specs=vmem,
        scratch_shapes=[
            pltpu.VMEM((n, F, T, R, L), jnp.float32),
            pltpu.VMEM((2, n, 3, T, L), jnp.float32),
            pltpu.VMEM((T, 4, R, L), jnp.int32),
            pltpu.VMEM((T, 4, R, L), jnp.int32),
            pltpu.VMEM((T, R, L), jnp.float32),
            pltpu.VMEM((R, T), jnp.int32),
            pltpu.VMEM((R, T), jnp.float32),
            dma(()), dma((2,)),
            dma((K, X - 1)), dma((K, X - 1)),
            dma((2, X)), dma((2, X)),
            dma((K, X)), dma((K, X)),
            dma((2, X)), dma((2, X)),
        ],
        compiler_params=pltpu.CompilerParams(collective_id=0, has_side_effects=True, vmem_limit_bytes=grant),
    )(*(pltpu.with_memory_space_constraint(v, pltpu.HBM) for v in (fields, shifts.T, courant.T)))


def solution(mesh):
    return jax.shard_map(
        shards,
        mesh=mesh,
        in_specs=(P(None, None, "rad", "az"), P(None, "rad"), P(None, "rad")),
        out_specs=P(None, None, "rad", "az"),
        check_vma=False,
    )
```

```python
import functools
import math

import jax
import jax.numpy as jnp
from jax import lax
from jax.experimental import pallas as pl
from jax.experimental.pallas import tpu as pltpu
from jax.sharding import PartitionSpec as P

inner_radius = 0.4
adiabatic = 1.4
MESH = pl.DeviceIdType.MESH
OFFSETS = (-2, -1, 0, 1)
CHUNKS = 4


def remote(src, dst, send, recv, az, rad):
    return pltpu.make_async_remote_copy(
        src_ref=src,
        dst_ref=dst,
        send_sem=send,
        recv_sem=recv,
        device_id={"az": az, "rad": rad},
        device_id_type=MESH,
    )


def minmod(a, b):
    return jnp.maximum(jnp.minimum(a, b), 0.0) + jnp.minimum(jnp.maximum(a, b), 0.0)


def kernel(n, rn, fields, shifts_in, courant_in, out, G, H, SEG, LANE, CA, shifts, courant,
           local_sem, small_sem, xs, xr, hs, hr, cs, cr, fs, fr):
    _, T, R, L = fields.shape
    X = n // 2
    K = xs.shape[0]
    tc = T // K
    az = lax.axis_index("az")
    rad = lax.axis_index("rad")
    x, c = az // 2, az % 2
    mate = x * 2 + (1 - c)

    def column(k):
        return lax.rem(x + k, X) * 2 + c

    def source(k, core):
        return lax.rem(x + X - k, X) * 2 + core

    has_low, has_high = rad > 0, rad < rn - 1
    sends = (has_high, has_low)
    receives = (has_low, has_high)
    toward = (rad + 1, rad - 1)

    local = pltpu.make_async_copy(fields, G.at[az], local_sem)
    local.start()
    small = (
        pltpu.make_async_copy(shifts_in, shifts, small_sem.at[0]),
        pltpu.make_async_copy(courant_in, courant, small_sem.at[1]),
    )
    for copy in small:
        copy.start()

    barrier = pltpu.get_barrier_semaphore()

    def greet(a, r):
        pl.semaphore_signal(barrier, inc=1, device_id={"az": a, "rad": r}, device_id_type=MESH)

    greet(mate, rad)
    for k in range(1, X):
        greet(column(k), rad)
    for way in range(2):
        @pl.when(sends[way])
        def _():
            for k in range(X):
                greet(column(k), toward[way])
    neighbours = has_low.astype(jnp.int32) + has_high.astype(jnp.int32)


    pl.semaphore_wait(barrier, X + X * neighbours)

    def block(ref, seg, j):
        return ref.at[seg, :, pl.ds(j * tc, tc)]

    def field_copy(j, k):
        return remote(fields.at[:, pl.ds(j * tc, tc)], block(G, az, j), xs.at[j, k - 1], xr.at[j, k - 1], column(k), rad)

    def field_arrival(j, k):
        seg = source(k, c)
        return remote(block(G, seg, j), block(G, seg, j), xs.at[j, k - 1], xr.at[j, k - 1], column(k), rad)

    def edge_copy(way, k):
        return remote(fields.at[0:3, :, (R - 1) * (1 - way), :], H.at[way, az], hs.at[way, k], hr.at[way, k], column(k), toward[way])

    def edge_arrival(way, k):
        return remote(H.at[way, az], H.at[way, source(k, c)], hs.at[way, k], hr.at[way, k], column(k), rad)

    def mate_copy(j, k):
        seg = source(k, c)
        sent = block(G, seg, j) if k else fields.at[:, pl.ds(j * tc, tc)]
        return remote(sent, block(G, seg, j), cs.at[j, k], cr.at[j, k], mate, rad)

    def mate_arrival(j, k):
        seg = source(k, 1 - c)
        return remote(block(G, seg, j), block(G, seg, j), cs.at[j, k], cr.at[j, k], mate, rad)

    def mate_edge(way, k):
        seg = source(k, c)
        return remote(H.at[way, seg], H.at[way, seg], fs.at[way, k], fr.at[way, k], mate, rad)

    def mate_edge_arrival(way, k):
        seg = source(k, 1 - c)
        return remote(H.at[way, seg], H.at[way, seg], fs.at[way, k], fr.at[way, k], mate, rad)

    for way in range(2):
        @pl.when(sends[way])
        def _():
            for k in range(X - 1, -1, -1):
                edge_copy(way, k).start()
    for j in range(K):
        for k in range(1, X):
            field_copy(j, k).start()
    for j in range(K):
        mate_copy(j, 0).start()

    for way in range(2):
        @pl.when(jnp.logical_not(receives[way]))
        def _():
            H[way] = jnp.zeros(H.shape[1:], jnp.float32)

    phi_count, rad_count = n * L, rn * R
    phi_step = 2.0 * math.pi / phi_count
    rad_step = 1.0 / rad_count
    spacing = min(rad_step, inner_radius * phi_step)
    dt = 0.2 * spacing
    viscosity = 0.05 * spacing * spacing / dt
    row = lax.broadcasted_iota(jnp.int32, (R, L), 0)
    lane = lax.broadcasted_iota(jnp.int32, (R, L), 1)
    radius = inner_radius + ((rad * R + row).astype(jnp.float32) + 0.5) * (1.0 / rad_count)
    width = radius * phi_step
    inv_r = 1.0 / radius
    inv_w = 1.0 / width
    spread_az = (dt * viscosity) * inv_w * inv_w
    spread_rad = dt * viscosity / (rad_step * rad_step)
    press_rad = dt * (adiabatic - 1.0) * 0.5 / rad_step
    press_az = (dt * (adiabatic - 1.0) * 0.5) * inv_w
    turn = dt * inv_r
    pull = dt * inv_r * inv_r
    heat = dt * (adiabatic - 1.0)
    heat_rad = heat * 0.5 / rad_step
    heat_az = (heat * 0.5) * inv_w
    heat_r = heat * inv_r
    bits = L.bit_length() - 1

    local.wait()
    for copy in small:
        copy.wait()
    for t in range(T):
        moves = jnp.broadcast_to(shifts[:, t : t + 1], (R, L))
        cour = jnp.broadcast_to(courant[:, t : t + 1], (R, L))
        CA[t] = jnp.abs(cour)
        sign = jnp.where(cour >= 0.0, 1, -1)
        for o, offset in enumerate(OFFSETS):
            s = moves - sign * offset
            s = jnp.where(s < 0, s + phi_count, s)
            s = jnp.where(s >= phi_count, s - phi_count, s)
            q = s >> bits
            rest = s & (L - 1)
            seg = az - q - jnp.where(lane + rest >= L, 1, 0)
            SEG[t, o] = jnp.where(seg < 0, seg + n, seg)
            LANE[t, o] = (lane - rest) & (L - 1)

    first_lane, last_lane = lane == 0, lane == L - 1
    low_own = (row == 0) & jnp.logical_not(has_low)
    high_own = (row == R - 1) & jnp.logical_not(has_high)
    low_halo = (row == 0) & has_low
    high_halo = (row == R - 1) & has_high

    def step(t, carry):
        raw = [[G[s, f, t] for f in range(4)] for s in range(n)]
        moved = []
        for s in range(n):
            before, here, after = raw[s - 1], raw[s], raw[(s + 1) % n]
            vr, vp, en, den = here

            def around(f):
                q = here[f]
                left = pltpu.roll(jnp.where(last_lane, before[f], q), 1, 1)
                right = pltpu.roll(jnp.where(first_lane, after[f], q), L - 1, 1)
                low = jnp.where(low_own, q, pltpu.roll(q, 1, 0))
                low = jnp.where(low_halo, H[0, s, f, pl.ds(t, 1), :], low)
                high = jnp.where(high_own, q, pltpu.roll(q, R - 1, 0))
                high = jnp.where(high_halo, H[1, s, f, pl.ds(t, 1), :], high)
                return left, right, low, high

            vl, vh, vd, vu = around(0)
            pl_, ph, pd, pu = around(1)
            el, eh, ed, eu = around(2)
            inv_den = 1.0 / den
            new_r = vr + (
                spread_az * (vh + vl - 2.0 * vr)
                + spread_rad * (vu + vd - 2.0 * vr)
                + (vp * vp * turn - pull)
                - press_rad * (eu - ed) * inv_den
            )
            new_p = vp + (
                spread_az * (ph + pl_ - 2.0 * vp)
                + spread_rad * (pu + pd - 2.0 * vp)
                - vr * vp * turn
                - press_az * (eh - el) * inv_den
            )
            new_e = en - en * (heat_rad * (vu - vd) + heat_az * (ph - pl_) + heat_r * vr)
            moved.append((new_r, new_p, new_e, den))
        amount = CA[t]
        half = 0.5 * (1.0 - amount)
        taken = [[] for _ in range(4)]
        for o in range(len(OFFSETS)):
            seg, at = SEG[t, o], LANE[t, o]
            chosen = [seg == s for s in range(n - 1)]
            for f in range(4):
                value = moved[n - 1][f]
                for s in range(n - 1):
                    value = jnp.where(chosen[s], moved[s][f], value)
                taken[f].append(jnp.take_along_axis(value, at, axis=1, mode="promise_in_bounds"))
        for f in range(4):
            q0, q1, q2, q3 = taken[f]
            d0, d1, d2 = q1 - q0, q2 - q1, q3 - q2
            enters = q1 + half * minmod(d0, d1)
            leaves = q2 + half * minmod(d1, d2)
            out[f, t] = q2 - amount * (leaves - enters)
        return carry

    def finish(j):
        for k in range(X):
            mate_arrival(j, k).wait_recv()
        def group(i, carry):
            for u in range(2):
                carry = step(2 * i + u, carry)
            return carry

        lax.fori_loop(j * (tc // 2), (j + 1) * (tc // 2), group, 0)

    for way in range(2):
        @pl.when(receives[way])
        def _():
            for k in range(X):
                edge_arrival(way, k).wait_recv()
                mate_edge(way, k).start()

    def turn_over(j, carry):
        @pl.when(j < K)
        def _():
            for k in range(1, X):
                field_arrival(j, k).wait_recv()
                mate_copy(j, k).start()

        for way in range(2):
            @pl.when((j == 1) & receives[way])
            def _():
                for k in range(X):
                    mate_edge_arrival(way, k).wait_recv()

        @pl.when(j > 0)
        def _():
            finish(j - 1)

        return carry

    lax.fori_loop(0, K + 1, turn_over, 0)

    for way in range(2):
        @pl.when(sends[way])
        def _():
            for k in range(X):
                edge_copy(way, k).wait_send()

        @pl.when(receives[way])
        def _():
            for k in range(X):
                mate_edge(way, k).wait_send()
    for j in range(K):
        for k in range(1, X):
            field_copy(j, k).wait_send()
        for k in range(X):
            mate_copy(j, k).wait_send()


def shards(fields, shifts, courant):
    n, rn = lax.axis_size("az"), lax.axis_size("rad")
    F, T, R, L = fields.shape
    X = n // 2
    K = math.gcd(T, CHUNKS)
    held = (n + 2) * F * T * R * L + 2 * n * 3 * T * L + 9 * T * R * L
    grant = 4 * held + (2 << 20)
    dma = pltpu.SemaphoreType.DMA
    vmem = pl.BlockSpec(memory_space=pltpu.VMEM)
    return pl.pallas_call(
        functools.partial(kernel, n, rn),
        out_shape=jax.ShapeDtypeStruct(fields.shape, jnp.float32),
        in_specs=[pl.BlockSpec(memory_space=pltpu.HBM)] * 3,
        out_specs=vmem,
        scratch_shapes=[
            pltpu.VMEM((n, F, T, R, L), jnp.float32),
            pltpu.VMEM((2, n, 3, T, L), jnp.float32),
            pltpu.VMEM((T, 4, R, L), jnp.int32),
            pltpu.VMEM((T, 4, R, L), jnp.int32),
            pltpu.VMEM((T, R, L), jnp.float32),
            pltpu.VMEM((R, T), jnp.int32),
            pltpu.VMEM((R, T), jnp.float32),
            dma(()), dma((2,)),
            dma((K, X - 1)), dma((K, X - 1)),
            dma((2, X)), dma((2, X)),
            dma((K, X)), dma((K, X)),
            dma((2, X)), dma((2, X)),
        ],
        compiler_params=pltpu.CompilerParams(collective_id=0, has_side_effects=True, vmem_limit_bytes=grant),
    )(*(pltpu.with_memory_space_constraint(v, pltpu.HBM) for v in (fields, shifts.T, courant.T)))


def solution(mesh):
    return jax.shard_map(
        shards,
        mesh=mesh,
        in_specs=(P(None, None, "rad", "az"), P(None, "rad"), P(None, "rad")),
        out_specs=P(None, None, "rad", "az"),
        check_vma=False,
    )
```
